32 devices in a mesh: seq: 16 (over z, y, core), tp: 2 (over x).
Axes of the slice: x: 2, y: 2, z: 4, core: 2. Of those that a mesh axis runs over, the one named last changes fastest.
Arguments:
- queries: bfloat16 [8192, 2048], P('seq', 'tp'), may hold values from -9 to 9
- keys: bfloat16 [8192, 2048], P('seq', 'tp'), may hold values from -9 to 9
- values: bfloat16 [8192, 2048], P('seq', 'tp'), may hold values from -6 to 6
- residual: bfloat16 [8192, 2048], P(('seq', 'tp')), may hold values from -36 to 36
- out_weight: bfloat16 [2048, 2048], P('tp'), may hold values from -0.125 to 0.125
- norm_gain: float32 [2048], replicated, may hold values from 0.25 to 1.75
- router: bfloat16 [2048, 8], replicated, may hold values from -0.25 to 0.25
- gate_weight: bfloat16 [2048, 5504], P('seq', 'tp'), may hold values from -0.125 to 0.125
- up_weight: bfloat16 [2048, 5504], P('seq', 'tp'), may hold values from -0.125 to 0.125
- down_weight: bfloat16 [5504, 2048], P('tp', 'seq'), may hold values from -0.078125 to 0.078125
- gate_shrink: bfloat16 [2048, 128], replicated, may hold values from -0.125 to 0.125
- up_shrink: bfloat16 [2048, 128], replicated, may hold values from -0.125 to 0.125
- gate_widen_maps: bfloat16 [128, 5504], P(None, 'tp'), may hold values from -0.75 to 0.75
- upward_widen_maps: bfloat16 [128, 5504], P(None, 'tp'), may hold values from -0.75 to 0.75
- down_shrink: bfloat16 [5504, 128], P('tp'), may hold values from -0.078125 to 0.078125
- down_expand: bfloat16 [128, 2048], replicated, may hold values from -1.5 to 1.5
- routing: int32 [8192, 2], P('seq'), may hold values from 0 to 7, all different within a row
- doc_lengths: int32 [4], replicated, may hold values from 1 to 4096, 8192 in all
Outputs:
- output: bfloat16 [8192, 2048], P(('seq', 'tp'))
The draws below stay inside these ranges and needn't reach their ends.
Inputs may be any that keep to these rules, and one draw needn't show every extreme that they name: `routing`: each row names two different experts. `doc_lengths`: the lengths sum to 8192.
All inputs are finite; a program needn't handle non-finite values.
Results may differ from the reference program's by a relative error of at most 0.015.
Values may be sent and summed in bfloat16 or wider, within the bound.
A program may use at most 128 MiB of HBM per device.

```python
import math
import jax
import jax.numpy as jnp
import numpy as np
from jax import lax

D = 2048
HEADS = 16
HEAD = 128
FF = 5504
EXPERTS = 8
RANK = 16
WINDOW = 4096
DOCS = 4
TOK_DEV = 512
TOKENS = 8192
LONGEST = 4096


def drawn_pair(key):
    full_shape = (TOKENS, HEADS * HEAD)
    base_keys = jnp.clip(jax.random.normal(jax.random.fold_in(key, 11), full_shape, jnp.float32), -6.0, 6.0)
    base_queries = jnp.clip(jax.random.normal(jax.random.fold_in(key, 12), full_shape, jnp.float32), -6.0, 6.0)
    return (base_queries, base_keys)


def draw_queries(key, part):
    return drawn_pair(key)[0].astype(jnp.bfloat16)


def draw_keys(key, part):
    return drawn_pair(key)[1].astype(jnp.bfloat16)


def draw_residual(key, part):
    drawn_draw = jnp.clip(jax.random.normal(jax.random.fold_in(key, 21), (TOKENS, D), jnp.float32), -4.0, 4.0)
    return drawn_draw.astype(jnp.bfloat16)


def shard_levels(stream_key, dims, cuts, smallest, high):
    def one(axis_at, shards_of):
        heights = jax.random.uniform(jax.random.fold_in(jax.random.fold_in(stream_key, 6), axis_at), (shards_of,), jnp.float32, smallest / len(cuts), high / len(cuts))
        return jnp.repeat(jnp.exp(heights), dims[axis_at] // shards_of).reshape((-1,) + (1,) * (len(dims) - axis_at - 1))

    level = one(*cuts[0])
    for cut in cuts[1:]:
        level = level * one(*cut)
    return level


def picks_of(rng, rows, amount, top, lift):
    order = jax.random.permutation(jax.random.fold_in(rng, 1), amount)
    boost = order
    for power in range(3):
        boost = boost * boost // amount
    boost = boost * lift // amount
    lots = jax.random.randint(jax.random.fold_in(rng, 2), (rows, amount), 0, 4096) + boost
    sure = jax.random.permutation(jax.random.fold_in(rng, 3), rows)[jnp.arange(amount) % rows]
    lots = jnp.where(jnp.arange(rows)[:, None] == sure[None, :], 1 << 14, lots)
    score = lots * amount + jnp.arange(amount)
    return lax.top_k(score.astype(jnp.int32), top)[1].astype(jnp.int32)


def length_profile(amount, total, most, slope):
    weights = [(1 << 20) // math.isqrt(standing ** slope) + 1 for standing in range(2, amount + 1)]
    surplus, holding = total - most - (amount - 1), [1] * (amount - 1)
    while surplus > 0:
        movable = [i for i in range(amount - 1) if holding[i] < most]
        mass, budget = sum([weights[i] for i in movable]), surplus
        for i in movable:
            addition = min(most - holding[i], max(1, budget * weights[i] // mass), surplus)
            holding[i] = holding[i] + addition
            surplus = surplus - addition
    return np.array([most] + holding)


def uneven_parts(stream_key, number_of, total, limit, lean):
    if number_of == 2:
        one = jax.random.randint(stream_key, (), max(1, total - limit), min(limit, total - 1) + 1)
        return jnp.stack([one, total - one])
    sizes = jnp.asarray(length_profile(number_of, total, limit, lean), jnp.int32)
    twos = (number_of - 1) // 2
    source_of, receiver = sizes[1:1 + 2 * twos:2], sizes[2:2 + 2 * twos:2]
    slack = jnp.minimum(source_of - 1, limit - receiver)
    moved = jax.random.randint(jax.random.fold_in(stream_key, 1), (twos,), 0, 1 << 20) % (slack + 1)
    sizes = sizes.at[1:1 + 2 * twos:2].set(source_of - moved).at[2:2 + 2 * twos:2].set(receiver + moved)
    return sizes[jax.random.permutation(jax.random.fold_in(stream_key, 2), number_of)]


def scatter_about(own_key, shape, deviation, most, split=(), held_as=jnp.bfloat16):
    entries = deviation * jax.random.normal(own_key, shape, jnp.float32)
    if split:
        entries = entries * shard_levels(own_key, shape, split, -0.22, 0.18)
    return jnp.clip(entries, -most, most).astype(held_as)


def setup_inputs(seed: int = 0) -> dict:
    streams_of = jax.random.split(jax.random.key(seed), 19)
    queries = draw_queries(jax.random.fold_in(streams_of[18], 71), 0)
    keys = draw_keys(jax.random.fold_in(streams_of[18], 71), 0)
    values = scatter_about(streams_of[2], (TOKENS, HEADS * HEAD), 1.0, 6.0, ((0, 16), (1, 2)))
    residual = draw_residual(jax.random.fold_in(streams_of[18], 71), 0)
    out_weight = scatter_about(streams_of[4], (HEADS * HEAD, D), (HEADS * HEAD) ** -0.5, 0.125, ((0, 2),))
    norm_gain = jnp.clip(1.0 + 0.15 * jax.random.normal(streams_of[5], (D,), jnp.float32), 0.25, 1.75)
    router = scatter_about(streams_of[6], (D, EXPERTS), (D // 4) ** -0.5, 0.25)
    gate_weight = scatter_about(streams_of[7], (D, FF), D ** -0.5, 0.125, ((0, 16), (1, 2)))
    up_weight = scatter_about(streams_of[8], (D, FF), D ** -0.5, 0.125, ((0, 16), (1, 2)))
    down_weight = scatter_about(streams_of[9], (FF, D), FF ** -0.5, 0.078125, ((0, 2), (1, 16)))
    gate_shrink = scatter_about(streams_of[10], (D, EXPERTS * RANK), D ** -0.5, 0.125)
    up_shrink = scatter_about(streams_of[11], (D, EXPERTS * RANK), D ** -0.5, 0.125)
    gate_widen_maps = scatter_about(streams_of[12], (EXPERTS * RANK, FF), (RANK * 4) ** -0.5, 0.75, ((1, 2),))
    upward_widen_maps = scatter_about(streams_of[13], (EXPERTS * RANK, FF), (RANK * 4) ** -0.5, 0.75, ((1, 2),))
    down_shrink = scatter_about(streams_of[14], (FF, EXPERTS * RANK), FF ** -0.5, 0.078125, ((0, 2),))
    down_expand = scatter_about(streams_of[15], (EXPERTS * RANK, D), RANK ** -0.5, 1.5)
    routing = picks_of(streams_of[16], TOKENS, EXPERTS, 2, 4096)
    doc_lengths = uneven_parts(streams_of[17], DOCS, TOKENS, LONGEST, 0).astype(jnp.int32)
    return dict(queries=queries, keys=keys, values=values, residual=residual, out_weight=out_weight, norm_gain=norm_gain, router=router, gate_weight=gate_weight, up_weight=up_weight, down_weight=down_weight, gate_shrink=gate_shrink, up_shrink=up_shrink, gate_widen_maps=gate_widen_maps, upward_widen_maps=upward_widen_maps, down_shrink=down_shrink, down_expand=down_expand, routing=routing, doc_lengths=doc_lengths)


adapter_scale_factor = 2.0
epsilon = 1e-05
masked_score = -1e+30

def document_of(positions, doc_ends):
    return lax.optimization_barrier(jnp.sum((positions[:, None] >= doc_ends[None, :]).astype(jnp.int32), axis=1))

def reference(queries, keys, values, residual, out_weight, norm_gain, router, gate_weight, up_weight, down_weight, gate_shrink, up_shrink, gate_widen_maps, upward_widen_maps, down_shrink, down_expand, routing, doc_lengths):
    total_width = HEADS * HEAD
    doc_ends = jnp.cumsum(doc_lengths).astype(jnp.int32)
    padded_keys = jnp.concatenate((jnp.zeros((WINDOW, total_width), keys.dtype), keys), axis=0)
    padded_values = jnp.concatenate((jnp.zeros((WINDOW, total_width), values.dtype), values), axis=0)
    score_scale = 1.0 / math.sqrt(HEAD)

    def attend_block(block_index):
        first_row = (block_index * TOK_DEV).astype(jnp.int32)
        query_block = lax.dynamic_slice(queries, (first_row, jnp.int32(0)), (TOK_DEV, total_width))
        key_block = lax.dynamic_slice(padded_keys, (first_row, jnp.int32(0)), (WINDOW + TOK_DEV, total_width))
        value_block = lax.dynamic_slice(padded_values, (first_row, jnp.int32(0)), (WINDOW + TOK_DEV, total_width))
        query_positions = first_row + jnp.arange(TOK_DEV, dtype=jnp.int32)
        key_positions = first_row - WINDOW + jnp.arange(WINDOW + TOK_DEV, dtype=jnp.int32)
        visible = key_positions[None, :] <= query_positions[:, None]
        visible = visible & (query_positions[:, None] - key_positions[None, :] < WINDOW)
        visible = visible & (key_positions[None, :] >= 0)
        visible = visible & (document_of(query_positions, doc_ends)[:, None] == document_of(key_positions, doc_ends)[None, :])
        query_heads = query_block.reshape(TOK_DEV, HEADS, HEAD).astype(jnp.float32)
        key_heads = key_block.reshape(WINDOW + TOK_DEV, HEADS, HEAD).astype(jnp.float32)
        value_heads = value_block.reshape(WINDOW + TOK_DEV, HEADS, HEAD).astype(jnp.float32)
        scores = jnp.einsum('qhd,khd->hqk', query_heads, key_heads) * score_scale
        scores = jnp.where(visible[None, :, :], scores, masked_score)
        largest = lax.optimization_barrier(jnp.max(scores, axis=2, keepdims=True))
        exponent = jnp.exp(scores - largest)
        attn_weights = (exponent / lax.optimization_barrier(jnp.sum(exponent, axis=2, keepdims=True))).astype(jnp.bfloat16)
        attended = jnp.einsum('hqk,khd->qhd', attn_weights.astype(jnp.float32), value_heads)
        return attended.reshape(TOK_DEV, total_width).astype(jnp.bfloat16)
    attended = lax.map(attend_block, jnp.arange(TOKENS // TOK_DEV, dtype=jnp.int32)).reshape(TOKENS, total_width)
    after_attention_state = residual.astype(jnp.float32) + jnp.dot(attended, out_weight, preferred_element_type=jnp.float32)
    mean_square = lax.optimization_barrier(jnp.mean(after_attention_state * after_attention_state, axis=1, keepdims=True))
    normed = (after_attention_state * lax.rsqrt(mean_square + epsilon) * norm_gain).astype(jnp.bfloat16)
    logits = jnp.dot(normed, router, preferred_element_type=jnp.float32)
    expert_ids = jnp.arange(EXPERTS, dtype=jnp.int32)
    first_logit = lax.optimization_barrier(jnp.sum(jnp.where(routing[:, 0:1] == expert_ids[None, :], logits, 0.0), axis=1))
    second_logit = lax.optimization_barrier(jnp.sum(jnp.where(routing[:, 1:2] == expert_ids[None, :], logits, 0.0), axis=1))
    weight_first = jax.nn.sigmoid(first_logit - second_logit)[:, None]
    weight_second = jax.nn.sigmoid(second_logit - first_logit)[:, None]
    rank_gate = jnp.dot(normed, gate_shrink, preferred_element_type=jnp.float32).astype(jnp.bfloat16)
    rank_up = jnp.dot(normed, up_shrink, preferred_element_type=jnp.float32).astype(jnp.bfloat16)
    frozen_gate_output = jnp.dot(normed, gate_weight, preferred_element_type=jnp.float32)
    frozen_up_output = jnp.dot(normed, up_weight, preferred_element_type=jnp.float32)
    column_expert = jnp.arange(EXPERTS * RANK, dtype=jnp.int32) // RANK
    hiddens = []
    pickers = []
    for slot_index in range(2):
        picker = column_expert[None, :] == routing[:, slot_index:slot_index + 1]
        pickers.append(picker)
        selected_gate_widen = jnp.where(picker, rank_gate, jnp.zeros_like(rank_gate))
        selected_upward_widen = jnp.where(picker, rank_up, jnp.zeros_like(rank_up))
        gate_complete_output = frozen_gate_output + adapter_scale_factor * jnp.dot(selected_gate_widen, gate_widen_maps, preferred_element_type=jnp.float32)
        upward_complete_output = frozen_up_output + adapter_scale_factor * jnp.dot(selected_upward_widen, upward_widen_maps, preferred_element_type=jnp.float32)
        hiddens.append(jax.nn.silu(gate_complete_output) * upward_complete_output)
    mixture = (weight_first * hiddens[0] + weight_second * hiddens[1]).astype(jnp.bfloat16)
    shrunk_first = jnp.dot(hiddens[0].astype(jnp.bfloat16), down_shrink, preferred_element_type=jnp.float32)
    shrunk_second = jnp.dot(hiddens[1].astype(jnp.bfloat16), down_shrink, preferred_element_type=jnp.float32)
    rank_down = weight_first * jnp.where(pickers[0], shrunk_first, 0.0) + weight_second * jnp.where(pickers[1], shrunk_second, 0.0)
    downward_adapter_term = jnp.dot(mixture, down_weight, preferred_element_type=jnp.float32)
    low_rank_product = jnp.dot(rank_down.astype(jnp.bfloat16), down_expand, preferred_element_type=jnp.float32)
    return (after_attention_state + downward_adapter_term + adapter_scale_factor * low_rank_product).astype(jnp.bfloat16)
```

```python
import functools
import math

import jax
import jax.numpy as jnp
from jax import lax
from jax.experimental import pallas as pl
from jax.experimental.pallas import tpu as pltpu
from jax.sharding import PartitionSpec as P

HEAD = 128
EXPERTS = 8
RANK = 16
WINDOW = 4096


adapter_scale_factor = 2.0
epsilon = 1e-05
masked_score = -1e30


MESH = pl.DeviceIdType.MESH
KEY_TILE = 512


def greet_all(n, me):
    barrier = pltpu.get_barrier_semaphore()

    def greet(i, carry):
        pl.semaphore_signal(
            barrier, inc=1, device_id={"seq": lax.rem(me + i, n)}, device_id_type=MESH
        )
        return carry

    lax.fori_loop(1, n, greet, 0)
    pl.semaphore_wait(barrier, n - 1)


def spread_kernel(n, group, q_ref, kv_ref, q_out, kv_out, kv_s, kv_r, q_s, q_r, f_s, f_r, own_s, own_r, loc):
    me = lax.axis_index("seq")
    chips = n // 2
    chip, core = me // 2, lax.rem(me, 2)
    sib = chip * 2 + (1 - core)
    tokens = q_ref.shape[0]
    part = tokens // group
    greet_all(n, me)

    def rows(j):
        return pl.ds(pl.multiple_of(j * tokens, tokens), tokens)

    def q_rows(j):
        return pl.ds(pl.multiple_of(j * part, part), part)

    def cols(d):
        return pl.ds(pl.multiple_of((d // group) * HEAD, HEAD), HEAD)

    def kv_copy(kind, source, d, send, recv):
        return pltpu.make_async_remote_copy(
            src_ref=kv_ref.at[kind, :, cols(d)],
            dst_ref=kv_out.at[kind, rows(source), :],
            send_sem=send,
            recv_sem=recv,
            device_id={"seq": d},
            device_id_type=MESH,
        )

    def q_copy(source, d, send, recv):
        return pltpu.make_async_remote_copy(
            src_ref=q_ref.at[q_rows(lax.rem(d, group)), cols(d)],
            dst_ref=q_out.at[q_rows(source), :],
            send_sem=send,
            recv_sem=recv,
            device_id={"seq": d},
            device_id_type=MESH,
        )

    def forward(kind, source, send, recv):
        return pltpu.make_async_remote_copy(
            src_ref=kv_out.at[kind, rows(source), :],
            dst_ref=kv_out.at[kind, rows(source), :],
            send_sem=send,
            recv_sem=recv,
            device_id={"seq": sib},
            device_id_type=MESH,
        )

    def send(c, carry):
        for b in range(2):
            d = lax.rem(chip + c, chips) * 2 + b
            kv_copy(b, me, d, kv_s.at[c, b], kv_r.at[c, core]).start()
            q_copy(me, d, q_s.at[c, b], q_r.at[c, core]).start()
        return carry

    lax.fori_loop(1, chips, send, 0)
    for kind in range(2):
        kv_copy(kind, me, sib, own_s.at[kind], own_r.at[kind]).start()
    q_copy(me, sib, own_s.at[2], own_r.at[2]).start()
    local = [
        pltpu.make_async_copy(kv_ref.at[kind, :, cols(me)], kv_out.at[kind, rows(me), :], loc.at[kind])
        for kind in range(2)
    ]
    local.append(
        pltpu.make_async_copy(
            q_ref.at[q_rows(lax.rem(me, group)), cols(me)], q_out.at[q_rows(me), :], loc.at[2]
        )
    )
    for copy in local:
        copy.start()

    def pass_on(c, carry):
        for b in range(2):
            source = lax.rem(chip - c + chips, chips) * 2 + b
            kv_copy(core, source, sib, kv_s.at[c, b], kv_r.at[c, b]).wait_recv()
            forward(core, source, f_s.at[c, b], f_r.at[c, b]).start()
        return carry

    lax.fori_loop(1, chips, pass_on, 0)

    def finish(c, carry):
        for b in range(2):
            d = lax.rem(chip + c, chips) * 2 + b
            source = lax.rem(chip - c + chips, chips) * 2 + b
            kv_copy(b, me, d, kv_s.at[c, b], kv_r.at[c, core]).wait_send()
            q_copy(me, d, q_s.at[c, b], q_r.at[c, core]).wait_send()
            q_copy(source, sib, q_s.at[c, b], q_r.at[c, b]).wait_recv()
            forward(core, source, f_s.at[c, b], f_r.at[c, b]).wait_send()
            forward(1 - core, source, f_s.at[c, b], f_r.at[c, b]).wait_recv()
        return carry

    lax.fori_loop(1, chips, finish, 0)
    for kind in range(2):
        kv_copy(kind, me, sib, own_s.at[kind], own_r.at[kind]).wait_send()
        kv_copy(kind, sib, sib, own_s.at[kind], own_r.at[kind]).wait_recv()
    q_copy(me, sib, own_s.at[2], own_r.at[2]).wait_send()
    q_copy(sib, sib, own_s.at[2], own_r.at[2]).wait_recv()
    for copy in local:
        copy.wait()


def spread(n, group, queries, stacked):
    tokens = queries.shape[0]
    chips = n // 2
    dma = pltpu.SemaphoreType.DMA
    return pl.pallas_call(
        functools.partial(spread_kernel, n, group),
        out_shape=(
            jax.ShapeDtypeStruct((n * tokens // group, HEAD), queries.dtype),
            jax.ShapeDtypeStruct((2, n * tokens, HEAD), queries.dtype),
        ),
        in_specs=[pl.BlockSpec(memory_space=pl.ANY)] * 2,
        out_specs=(pl.BlockSpec(memory_space=pl.ANY),) * 2,
        scratch_shapes=[dma((chips, 2))] * 6 + [dma((3,))] * 3,
        compiler_params=pltpu.CompilerParams(collective_id=0, has_side_effects=True),
        cost_estimate=pl.CostEstimate(flops=0, bytes_accessed=200_000_000, transcendentals=0),
        name="spread_heads",
    )(queries, stacked)


def gather_kernel(n, group, x_ref, out_ref, s_sem, r_sem, loc):
    me = lax.axis_index("seq")
    tokens = out_ref.shape[0]
    part = tokens // group
    greet_all(n, me)

    def place(source):
        return out_ref.at[
            pl.ds(pl.multiple_of(lax.rem(source, group) * part, part), part),
            pl.ds(pl.multiple_of((source // group) * HEAD, HEAD), HEAD),
        ]

    def piece(d):
        return x_ref.at[pl.ds(pl.multiple_of(d * part, part), part), :]

    def copy(i, source, d):
        return pltpu.make_async_remote_copy(
            src_ref=piece(d),
            dst_ref=place(source),
            send_sem=s_sem.at[i],
            recv_sem=r_sem.at[i],
            device_id={"seq": d},
            device_id_type=MESH,
        )

    def send(i, carry):
        copy(i, me, lax.rem(me + i, n)).start()
        return carry

    lax.fori_loop(1, n, send, 0)
    own = pltpu.make_async_copy(piece(me), place(me), loc)
    own.start()

    def finish(i, carry):
        d = lax.rem(me + i, n)
        copy(i, me, d).wait_send()
        copy(i, lax.rem(me - i + n, n), d).wait_recv()
        return carry

    lax.fori_loop(1, n, finish, 0)
    own.wait()


def regather(n, group, heads, tokens, attended):
    dma = pltpu.SemaphoreType.DMA
    return pl.pallas_call(
        functools.partial(gather_kernel, n, group),
        out_shape=jax.ShapeDtypeStruct((tokens, heads * HEAD), attended.dtype),
        in_specs=[pl.BlockSpec(memory_space=pl.ANY)],
        out_specs=pl.BlockSpec(memory_space=pl.ANY),
        scratch_shapes=[dma((n,)), dma((n,)), dma],
        compiler_params=pltpu.CompilerParams(collective_id=1, has_side_effects=True),
        cost_estimate=pl.CostEstimate(flops=0, bytes_accessed=60_000_000, transcendentals=0),
        name="regather_heads",
    )(attended)


def attend_kernel(tokens, part, docs, scalars, q_ref, k_ref, v_ref, o_ref):
    block = pl.program_id(0)
    first = block * tokens + scalars[docs] * part
    last = first + part - 1
    start = jnp.int32(0)
    q_pos = first + lax.broadcasted_iota(jnp.int32, (part, 1), 0)
    low = jnp.maximum(q_pos - (WINDOW - 1), 0)
    for j in range(docs):
        end = scalars[j]
        start = jnp.where(first >= end, end, start)
        low = jnp.maximum(low, jnp.where(q_pos >= end, end, 0))
    start = jnp.maximum(start, jnp.maximum(first - (WINDOW - 1), 0))
    q = q_ref[...]
    scale = 1.0 / math.sqrt(HEAD)

    def step(tile, carry):
        m, total, acc = carry
        base = pl.multiple_of(tile * KEY_TILE, KEY_TILE)
        k = k_ref[pl.ds(base, KEY_TILE), :]
        v = v_ref[pl.ds(base, KEY_TILE), :]
        scores = lax.dot_general(
            q, k, (((1,), (1,)), ((), ())), preferred_element_type=jnp.float32
        ) * scale
        k_pos = base + lax.broadcasted_iota(jnp.int32, (part, KEY_TILE), 1)
        scores = jnp.where((k_pos >= low) & (k_pos <= q_pos), scores, masked_score)
        new_m = jnp.maximum(m, jnp.max(scores, axis=1, keepdims=True))
        weights = jnp.exp(scores - new_m)
        shrink = jnp.exp(m - new_m)
        total = total * shrink + jnp.sum(weights, axis=1, keepdims=True)
        acc = acc * shrink + jnp.dot(
            weights.astype(jnp.bfloat16), v, preferred_element_type=jnp.float32
        )
        return new_m, total, acc

    _, total, acc = lax.fori_loop(
        start // KEY_TILE,
        last // KEY_TILE + 1,
        step,
        (
            jnp.full((part, 1), masked_score, jnp.float32),
            jnp.zeros((part, 1), jnp.float32),
            jnp.zeros((part, HEAD), jnp.float32),
        ),
    )
    o_ref[...] = (acc / total).astype(o_ref.dtype)


def attend(n, tokens, part, docs, scalars, q, kv):
    return pl.pallas_call(
        functools.partial(attend_kernel, tokens, part, docs),
        out_shape=jax.ShapeDtypeStruct(q.shape, q.dtype),
        grid_spec=pltpu.PrefetchScalarGridSpec(
            num_scalar_prefetch=1,
            grid=(n,),
            in_specs=[
                pl.BlockSpec((part, HEAD), lambda i, s: (i, 0)),
                pl.BlockSpec((None, n * tokens, HEAD), lambda i, s: (0, 0, 0)),
                pl.BlockSpec((None, n * tokens, HEAD), lambda i, s: (1, 0, 0)),
            ],
            out_specs=pl.BlockSpec((part, HEAD), lambda i, s: (i, 0)),
        ),
        compiler_params=pltpu.CompilerParams(vmem_limit_bytes=40 * 1024 * 1024),
        cost_estimate=pl.CostEstimate(
            flops=20_000_000_000, bytes_accessed=8_000_000, transcendentals=20_000_000
        ),
        name="attend_docs",
    )(scalars, q, kv, kv)


def sum_rows(partial, axis):
    count = lax.axis_size(axis)
    if count != 2:
        return lax.psum_scatter(
            partial.astype(jnp.bfloat16), axis, scatter_dimension=0, tiled=True
        ).astype(jnp.float32)
    half = partial.shape[0] // 2
    me = lax.axis_index(axis)
    away = lax.dynamic_slice_in_dim(partial, (1 - me) * half, half, 0)
    here = lax.dynamic_slice_in_dim(partial, me * half, half, 0)
    come = lax.ppermute(away.astype(jnp.bfloat16), axis, [(0, 1), (1, 0)])
    return here.astype(jnp.float32) + come.astype(jnp.float32)


def all_rows(own, axis):
    count = lax.axis_size(axis)
    if count != 2:
        return lax.all_gather(own, axis, axis=0, tiled=True)
    come = lax.ppermute(own, axis, [(0, 1), (1, 0)])
    first = lax.axis_index(axis) == 0
    return jnp.concatenate((jnp.where(first, own, come), jnp.where(first, come, own)), axis=0)


def on_device(
    queries,
    keys,
    values,
    residual,
    out_weight,
    norm_gain,
    router,
    gate_weight,
    up_weight,
    down_weight,
    gate_shrink,
    up_shrink,
    gate_widen_maps,
    upward_widen_maps,
    down_shrink,
    down_expand,
    routing,
    doc_lengths,
):
    tokens_here = queries.shape[0]
    total_width = queries.shape[1]
    heads_here = total_width // HEAD
    seq_count = lax.axis_size("seq")
    group = seq_count // heads_here
    part = tokens_here // group
    seq_index = lax.axis_index("seq")
    stacked = jnp.stack((keys, values))
    head_queries, head_kv = spread(seq_count, group, queries, stacked)
    doc_ends = jnp.cumsum(doc_lengths)
    scalars = jnp.concatenate((doc_ends, lax.rem(seq_index, group)[None])).astype(jnp.int32)
    attended = attend(
        seq_count, tokens_here, part, doc_lengths.shape[0], scalars, head_queries, head_kv
    )
    attended = regather(seq_count, group, heads_here, tokens_here, attended)
    projected = sum_rows(
        jnp.dot(attended, out_weight, preferred_element_type=jnp.float32), "tp"
    )
    after_attention_state = residual.astype(jnp.float32) + projected
    mean_square = jnp.mean(after_attention_state * after_attention_state, axis=1, keepdims=True)
    normed_own = (after_attention_state * lax.rsqrt(mean_square + epsilon) * norm_gain).astype(
        jnp.bfloat16
    )
    normed = all_rows(normed_own, "tp")
    rank_gate = jnp.dot(normed, gate_shrink, preferred_element_type=jnp.float32).astype(
        jnp.bfloat16
    )
    rank_up = jnp.dot(normed, up_shrink, preferred_element_type=jnp.float32).astype(jnp.bfloat16)
    logits = jnp.dot(normed, router, preferred_element_type=jnp.float32)
    expert_ids = jnp.arange(EXPERTS, dtype=jnp.int32)
    first_logit = jnp.sum(jnp.where(routing[:, 0:1] == expert_ids[None, :], logits, 0.0), axis=1)
    second_logit = jnp.sum(jnp.where(routing[:, 1:2] == expert_ids[None, :], logits, 0.0), axis=1)
    weight_first = jax.nn.sigmoid(first_logit - second_logit)[:, None]
    weight_second = jax.nn.sigmoid(second_logit - first_logit)[:, None]
    frozen_gate_output = jnp.dot(
        normed,
        lax.all_gather(gate_weight, "seq", axis=0, tiled=True),
        preferred_element_type=jnp.float32,
    )
    frozen_up_output = jnp.dot(
        normed,
        lax.all_gather(up_weight, "seq", axis=0, tiled=True),
        preferred_element_type=jnp.float32,
    )
    column_expert = jnp.arange(EXPERTS * RANK, dtype=jnp.int32) // RANK
    hiddens = []
    pickers = []
    for slot_index in range(2):
        picker = column_expert[None, :] == routing[:, slot_index : slot_index + 1]
        pickers.append(picker)
        selected_gate_widen = jnp.where(picker, rank_gate, jnp.zeros_like(rank_gate))
        selected_upward_widen = jnp.where(picker, rank_up, jnp.zeros_like(rank_up))
        gate_complete_output = frozen_gate_output + adapter_scale_factor * jnp.dot(
            selected_gate_widen, gate_widen_maps, preferred_element_type=jnp.float32
        )
        upward_complete_output = frozen_up_output + adapter_scale_factor * jnp.dot(
            selected_upward_widen, upward_widen_maps, preferred_element_type=jnp.float32
        )
        hiddens.append(jax.nn.silu(gate_complete_output) * upward_complete_output)
    mixture = (weight_first * hiddens[0] + weight_second * hiddens[1]).astype(jnp.bfloat16)
    shrunk_first = jnp.dot(
        hiddens[0].astype(jnp.bfloat16), down_shrink, preferred_element_type=jnp.float32
    )
    shrunk_second = jnp.dot(
        hiddens[1].astype(jnp.bfloat16), down_shrink, preferred_element_type=jnp.float32
    )
    rank_down = weight_first * jnp.where(pickers[0], shrunk_first, 0.0) + weight_second * jnp.where(
        pickers[1], shrunk_second, 0.0
    )
    downward_adapter_term = jnp.dot(
        mixture,
        lax.all_gather(down_weight, "seq", axis=1, tiled=True),
        preferred_element_type=jnp.float32,
    )
    downward_token_rows = sum_rows(downward_adapter_term, "tp")
    rank_rows = sum_rows(rank_down, "tp")
    low_rank_product = jnp.dot(
        rank_rows.astype(jnp.bfloat16), down_expand, preferred_element_type=jnp.float32
    )
    return (
        after_attention_state + downward_token_rows + adapter_scale_factor * low_rank_product
    ).astype(jnp.bfloat16)


def solution(mesh):
    placed = (
        P("seq", "tp"),
        P("seq", "tp"),
        P("seq", "tp"),
        P(("seq", "tp"), None),
        P("tp", None),
        P(),
        P(),
        P("seq", "tp"),
        P("seq", "tp"),
        P("tp", "seq"),
        P(),
        P(),
        P(None, "tp"),
        P(None, "tp"),
        P("tp", None),
        P(),
        P("seq", None),
        P(),
    )
    return jax.shard_map(
        on_device, mesh=mesh, in_specs=placed, out_specs=P(("seq", "tp"), None), check_vma=False
    )
```

```python
import functools
import math

import jax
import jax.numpy as jnp
from jax import lax
from jax.experimental import pallas as pl
from jax.experimental.pallas import tpu as pltpu
from jax.sharding import PartitionSpec as P

HEAD = 128
EXPERTS = 8
RANK = 16
WINDOW = 4096


adapter_scale_factor = 2.0
epsilon = 1e-05
masked_score = -1e30


MESH = pl.DeviceIdType.MESH
KEY_TILE = 512


def greet_all(n, me):
    barrier = pltpu.get_barrier_semaphore()

    def greet(i, carry):
        pl.semaphore_signal(
            barrier, inc=1, device_id={"seq": lax.rem(me + i, n)}, device_id_type=MESH
        )
        return carry

    lax.fori_loop(1, n, greet, 0)
    pl.semaphore_wait(barrier, n - 1)


def spread_kernel(n, group, q_ref, kv_ref, q_out, kv_out, kv_s, kv_r, q_s, q_r, f_s, f_r, own_s, own_r, loc):
    me = lax.axis_index("seq")
    chips = n // 2
    chip, core = me // 2, lax.rem(me, 2)
    sib = chip * 2 + (1 - core)
    tokens = q_ref.shape[0]
    part = tokens // group
    greet_all(n, me)

    def rows(j):
        return pl.ds(pl.multiple_of(j * tokens, tokens), tokens)

    def q_rows(j):
        return pl.ds(pl.multiple_of(j * part, part), part)

    def cols(d):
        return pl.ds(pl.multiple_of((d // group) * HEAD, HEAD), HEAD)

    def kv_copy(kind, source, d, send, recv):
        return pltpu.make_async_remote_copy(
            src_ref=kv_ref.at[kind, :, cols(d)],
            dst_ref=kv_out.at[kind, rows(source), :],
            send_sem=send,
            recv_sem=recv,
            device_id={"seq": d},
            device_id_type=MESH,
        )

    def q_copy(source, d, send, recv):
        return pltpu.make_async_remote_copy(
            src_ref=q_ref.at[q_rows(lax.rem(d, group)), cols(d)],
            dst_ref=q_out.at[q_rows(source), :],
            send_sem=send,
            recv_sem=recv,
            device_id={"seq": d},
            device_id_type=MESH,
        )

    def forward(kind, source, send, recv):
        return pltpu.make_async_remote_copy(
            src_ref=kv_out.at[kind, rows(source), :],
            dst_ref=kv_out.at[kind, rows(source), :],
            send_sem=send,
            recv_sem=recv,
            device_id={"seq": sib},
            device_id_type=MESH,
        )

    def send(c, carry):
        for b in range(2):
            d = lax.rem(chip + c, chips) * 2 + b
            kv_copy(b, me, d, kv_s.at[c, b], kv_r.at[c, core]).start()
            q_copy(me, d, q_s.at[c, b], q_r.at[c, core]).start()
        return carry

    lax.fori_loop(1, chips, send, 0)
    for kind in range(2):
        kv_copy(kind, me, sib, own_s.at[kind], own_r.at[kind]).start()
    q_copy(me, sib, own_s.at[2], own_r.at[2]).start()
    local = [
        pltpu.make_async_copy(kv_ref.at[kind, :, cols(me)], kv_out.at[kind, rows(me), :], loc.at[kind])
        for kind in range(2)
    ]
    local.append(
        pltpu.make_async_copy(
            q_ref.at[q_rows(lax.rem(me, group)), cols(me)], q_out.at[q_rows(me), :], loc.at[2]
        )
    )
    for copy in local:
        copy.start()

    def pass_on(c, carry):
        for b in range(2):
            source = lax.rem(chip - c + chips, chips) * 2 + b
            kv_copy(core, source, sib, kv_s.at[c, b], kv_r.at[c, b]).wait_recv()
            forward(core, source, f_s.at[c, b], f_r.at[c, b]).start()
        return carry

    lax.fori_loop(1, chips, pass_on, 0)

    def finish(c, carry):
        for b in range(2):
            d = lax.rem(chip + c, chips) * 2 + b
            source = lax.rem(chip - c + chips, chips) * 2 + b
            kv_copy(b, me, d, kv_s.at[c, b], kv_r.at[c, core]).wait_send()
            q_copy(me, d, q_s.at[c, b], q_r.at[c, core]).wait_send()
            q_copy(source, sib, q_s.at[c, b], q_r.at[c, b]).wait_recv()
            forward(core, source, f_s.at[c, b], f_r.at[c, b]).wait_send()
            forward(1 - core, source, f_s.at[c, b], f_r.at[c, b]).wait_recv()
        return carry

    lax.fori_loop(1, chips, finish, 0)
    for kind in range(2):
        kv_copy(kind, me, sib, own_s.at[kind], own_r.at[kind]).wait_send()
        kv_copy(kind, sib, sib, own_s.at[kind], own_r.at[kind]).wait_recv()
    q_copy(me, sib, own_s.at[2], own_r.at[2]).wait_send()
    q_copy(sib, sib, own_s.at[2], own_r.at[2]).wait_recv()
    for copy in local:
        copy.wait()


def spread(n, group, queries, stacked):
    tokens = queries.shape[0]
    chips = n // 2
    dma = pltpu.SemaphoreType.DMA
    return pl.pallas_call(
        functools.partial(spread_kernel, n, group),
        out_shape=(
            jax.ShapeDtypeStruct((n * tokens // group, HEAD), queries.dtype),
            jax.ShapeDtypeStruct((2, n * tokens, HEAD), queries.dtype),
        ),
        in_specs=[pl.BlockSpec(memory_space=pl.ANY)] * 2,
        out_specs=(pl.BlockSpec(memory_space=pl.ANY),) * 2,
        scratch_shapes=[dma((chips, 2))] * 6 + [dma((3,))] * 3,
        compiler_params=pltpu.CompilerParams(collective_id=0, has_side_effects=True),
        cost_estimate=pl.CostEstimate(flops=0, bytes_accessed=200_000_000, transcendentals=0),
        name="spread_heads",
    )(queries, stacked)


def gather_kernel(n, tn, group, heads, rotate, x_ref, out_ref, s_sem, r_sem, loc):
    me, mt = lax.axis_index("seq"), lax.axis_index("tp")
    kept = out_ref.shape[0]
    part = kept * tn // group
    per = kept // part
    head, sub = me // group, lax.rem(me, group)
    owner = sub // per
    mine = owner == mt
    sources = tn * heads * per

    def source_of(i):
        t, h, q = i // (heads * per), lax.rem(i // per, heads), lax.rem(i, per)
        return h * group + mt * per + q, t

    def place(h, q, t, u):
        slot = lax.rem(t - u + tn, tn) if rotate else t
        return out_ref.at[
            pl.ds(pl.multiple_of(q * part, part), part),
            pl.ds(pl.multiple_of((slot * heads + h) * HEAD, HEAD), HEAD),
        ]

    def piece(d):
        return x_ref.at[pl.ds(pl.multiple_of(d * part, part), part), :]

    barrier = pltpu.get_barrier_semaphore()

    def greet(i, carry):
        s, t = source_of(i)

        @pl.when((s != me) | (t != mt))
        def _():
            pl.semaphore_signal(barrier, inc=1, device_id={"seq": s, "tp": t}, device_id_type=MESH)

        return carry

    lax.fori_loop(0, sources, greet, 0)
    pl.semaphore_wait(barrier, n - jnp.where(mine, 1, 0))
    own_id = (mt * heads + head) * per + lax.rem(sub, per)

    def send_copy(d):
        return pltpu.make_async_remote_copy(
            src_ref=piece(d),
            dst_ref=place(head, lax.rem(sub, per), mt, owner),
            send_sem=s_sem.at[d],
            recv_sem=r_sem.at[own_id],
            device_id={"seq": d, "tp": owner},
            device_id_type=MESH,
        )

    def receive(i):
        t, h, q = i // (heads * per), lax.rem(i // per, heads), lax.rem(i, per)
        return pltpu.make_async_remote_copy(
            src_ref=piece(me),
            dst_ref=place(h, q, t, mt),
            send_sem=s_sem.at[me],
            recv_sem=r_sem.at[i],
            device_id={"seq": lax.rem(me + 1, n), "tp": owner},
            device_id_type=MESH,
        )

    own = pltpu.make_async_copy(piece(me), place(head, lax.rem(sub, per), mt, mt), loc)

    def send(i, carry):
        send_copy(lax.rem(me + i, n)).start()
        return carry

    lax.fori_loop(1, n, send, 0)

    @pl.when(mine)
    def _():
        own.start()

    @pl.when(jnp.logical_not(mine))
    def _():
        send_copy(me).start()

    def sent(i, carry):
        send_copy(lax.rem(me + i, n)).wait_send()
        return carry

    lax.fori_loop(1, n, sent, 0)

    def arrive(i, carry):
        s, t = source_of(i)

        @pl.when((s != me) | (t != mt))
        def _():
            receive(i).wait_recv()

        return carry

    lax.fori_loop(0, sources, arrive, 0)

    @pl.when(mine)
    def _():
        own.wait()

    @pl.when(jnp.logical_not(mine))
    def _():
        send_copy(me).wait_send()


def regather(n, tn, group, heads, tokens, attended):
    dma = pltpu.SemaphoreType.DMA
    kept = tokens // tn
    part = tokens // group
    assert kept % part == 0
    return pl.pallas_call(
        functools.partial(gather_kernel, n, tn, group, heads, tn == 2),
        out_shape=jax.ShapeDtypeStruct((kept, tn * heads * HEAD), attended.dtype),
        in_specs=[pl.BlockSpec(memory_space=pl.ANY)],
        out_specs=pl.BlockSpec(memory_space=pl.ANY),
        scratch_shapes=[dma((n,)), dma((tn * heads * (kept // part),)), dma],
        compiler_params=pltpu.CompilerParams(collective_id=1, has_side_effects=True),
        cost_estimate=pl.CostEstimate(flops=0, bytes_accessed=60_000_000, transcendentals=0),
        name="regather_heads",
    )(attended)


def attend_kernel(tokens, part, docs, scalars, q_ref, k_ref, v_ref, o_ref):
    block = pl.program_id(0)
    first = block * tokens + scalars[docs] * part
    last = first + part - 1
    start = jnp.int32(0)
    q_pos = first + lax.broadcasted_iota(jnp.int32, (part, 1), 0)
    low = jnp.maximum(q_pos - (WINDOW - 1), 0)
    for j in range(docs):
        end = scalars[j]
        start = jnp.where(first >= end, end, start)
        low = jnp.maximum(low, jnp.where(q_pos >= end, end, 0))
    start = jnp.maximum(start, jnp.maximum(first - (WINDOW - 1), 0))
    q = q_ref[...]
    scale = 1.0 / math.sqrt(HEAD)

    def step(tile, carry):
        m, total, acc = carry
        base = pl.multiple_of(tile * KEY_TILE, KEY_TILE)
        k = k_ref[pl.ds(base, KEY_TILE), :]
        v = v_ref[pl.ds(base, KEY_TILE), :]
        scores = lax.dot_general(
            q, k, (((1,), (1,)), ((), ())), preferred_element_type=jnp.float32
        ) * scale
        k_pos = base + lax.broadcasted_iota(jnp.int32, (part, KEY_TILE), 1)
        scores = jnp.where((k_pos >= low) & (k_pos <= q_pos), scores, masked_score)
        new_m = jnp.maximum(m, jnp.max(scores, axis=1, keepdims=True))
        weights = jnp.exp(scores - new_m)
        shrink = jnp.exp(m - new_m)
        total = total * shrink + jnp.sum(weights, axis=1, keepdims=True)
        acc = acc * shrink + jnp.dot(
            weights.astype(jnp.bfloat16), v, preferred_element_type=jnp.float32
        )
        return new_m, total, acc

    _, total, acc = lax.fori_loop(
        start // KEY_TILE,
        last // KEY_TILE + 1,
        step,
        (
            jnp.full((part, 1), masked_score, jnp.float32),
            jnp.zeros((part, 1), jnp.float32),
            jnp.zeros((part, HEAD), jnp.float32),
        ),
    )
    o_ref[...] = (acc / total).astype(o_ref.dtype)


def attend(n, tokens, part, docs, scalars, q, kv):
    return pl.pallas_call(
        functools.partial(attend_kernel, tokens, part, docs),
        out_shape=jax.ShapeDtypeStruct(q.shape, q.dtype),
        grid_spec=pltpu.PrefetchScalarGridSpec(
            num_scalar_prefetch=1,
            grid=(n,),
            in_specs=[
                pl.BlockSpec((part, HEAD), lambda i, s: (i, 0)),
                pl.BlockSpec((None, n * tokens, HEAD), lambda i, s: (0, 0, 0)),
                pl.BlockSpec((None, n * tokens, HEAD), lambda i, s: (1, 0, 0)),
            ],
            out_specs=pl.BlockSpec((part, HEAD), lambda i, s: (i, 0)),
        ),
        compiler_params=pltpu.CompilerParams(vmem_limit_bytes=40 * 1024 * 1024),
        cost_estimate=pl.CostEstimate(
            flops=20_000_000_000, bytes_accessed=8_000_000, transcendentals=20_000_000
        ),
        name="attend_docs",
    )(scalars, q, kv, kv)


def dot_t(rows, other):
    return lax.dot_general(
        rows, other, (((1,), (1,)), ((), ())), preferred_element_type=jnp.float32
    )


def feed_forward(normed, routing, weights, router, gate_shrink, up_shrink, gate_widen_maps, upward_widen_maps, down_shrink):
    rank_gate = jnp.dot(normed, gate_shrink, preferred_element_type=jnp.float32).astype(
        jnp.bfloat16
    )
    rank_up = jnp.dot(normed, up_shrink, preferred_element_type=jnp.float32).astype(jnp.bfloat16)
    logits = jnp.dot(normed, router, preferred_element_type=jnp.float32)
    expert_ids = jnp.arange(EXPERTS, dtype=jnp.int32)
    first_logit = jnp.sum(jnp.where(routing[:, 0:1] == expert_ids[None, :], logits, 0.0), axis=1)
    second_logit = jnp.sum(jnp.where(routing[:, 1:2] == expert_ids[None, :], logits, 0.0), axis=1)
    weight_first = jax.nn.sigmoid(first_logit - second_logit)[:, None]
    weight_second = jax.nn.sigmoid(second_logit - first_logit)[:, None]
    frozen_gate_output = dot_t(normed, weights[0])
    frozen_up_output = dot_t(normed, weights[1])
    column_expert = jnp.arange(EXPERTS * RANK, dtype=jnp.int32) // RANK
    hiddens = []
    pickers = []
    for slot_index in range(2):
        picker = column_expert[None, :] == routing[:, slot_index : slot_index + 1]
        pickers.append(picker)
        selected_gate_widen = jnp.where(picker, rank_gate, jnp.zeros_like(rank_gate))
        selected_upward_widen = jnp.where(picker, rank_up, jnp.zeros_like(rank_up))
        gate_complete_output = frozen_gate_output + adapter_scale_factor * jnp.dot(
            selected_gate_widen, gate_widen_maps, preferred_element_type=jnp.float32
        )
        upward_complete_output = frozen_up_output + adapter_scale_factor * jnp.dot(
            selected_upward_widen, upward_widen_maps, preferred_element_type=jnp.float32
        )
        hiddens.append(jax.nn.silu(gate_complete_output) * upward_complete_output)
    mixture = (weight_first * hiddens[0] + weight_second * hiddens[1]).astype(jnp.bfloat16)
    shrunk_first = jnp.dot(
        hiddens[0].astype(jnp.bfloat16), down_shrink, preferred_element_type=jnp.float32
    )
    shrunk_second = jnp.dot(
        hiddens[1].astype(jnp.bfloat16), down_shrink, preferred_element_type=jnp.float32
    )
    rank_down = weight_first * jnp.where(pickers[0], shrunk_first, 0.0) + weight_second * jnp.where(
        pickers[1], shrunk_second, 0.0
    )
    downward_adapter_term = jnp.dot(
        mixture,
        weights[2],
        preferred_element_type=jnp.float32,
    )
    return downward_adapter_term.astype(jnp.bfloat16), rank_down.astype(jnp.bfloat16)

def on_device(
    queries,
    keys,
    values,
    residual,
    out_weight,
    norm_gain,
    router,
    gate_weight,
    up_weight,
    down_weight,
    gate_shrink,
    up_shrink,
    gate_widen_maps,
    upward_widen_maps,
    down_shrink,
    down_expand,
    routing,
    doc_lengths,
):
    tokens_here = queries.shape[0]
    total_width = queries.shape[1]
    heads_here = total_width // HEAD
    seq_count = lax.axis_size("seq")
    group = seq_count // heads_here
    part = tokens_here // group
    seq_index = lax.axis_index("seq")
    tp_count = lax.axis_size("tp")
    weights = lax.all_gather(
        jnp.stack((gate_weight.T, up_weight.T, down_weight)), "seq", axis=2, tiled=True
    )
    stacked = jnp.stack((keys, values))
    head_queries, head_kv = spread(seq_count, group, queries, stacked)
    doc_ends = jnp.cumsum(doc_lengths)
    scalars = jnp.concatenate((doc_ends, lax.rem(seq_index, group)[None])).astype(jnp.int32)
    attended = attend(
        seq_count, tokens_here, part, doc_lengths.shape[0], scalars, head_queries, head_kv
    )
    attended = regather(seq_count, tp_count, group, heads_here, tokens_here, attended)
    if tp_count == 2:
        out_other = lax.ppermute(out_weight, "tp", [(0, 1), (1, 0)])
        projected = jnp.dot(
            attended[:, :total_width], out_weight, preferred_element_type=jnp.float32
        ) + jnp.dot(attended[:, total_width:], out_other, preferred_element_type=jnp.float32)
    else:
        projected = jnp.dot(
            attended,
            lax.all_gather(out_weight, "tp", axis=0, tiled=True),
            preferred_element_type=jnp.float32,
        )
    after_attention_state = residual.astype(jnp.float32) + projected
    mean_square = jnp.mean(after_attention_state * after_attention_state, axis=1, keepdims=True)
    normed_own = (after_attention_state * lax.rsqrt(mean_square + epsilon) * norm_gain).astype(
        jnp.bfloat16
    )
    shared = (router, gate_shrink, up_shrink, gate_widen_maps, upward_widen_maps, down_shrink)
    if tp_count == 2:
        swap = [(0, 1), (1, 0)]
        half = tokens_here // 2
        me = lax.axis_index("tp")
        normed_away = lax.ppermute(normed_own, "tp", swap)
        routing_own = lax.dynamic_slice_in_dim(routing, me * half, half, 0)
        routing_away = lax.dynamic_slice_in_dim(routing, (1 - me) * half, half, 0)
        away = feed_forward(normed_away, routing_away, weights, *shared)
        come = [lax.ppermute(part_sum, "tp", swap) for part_sum in away]
        normed_own, _ = lax.optimization_barrier((normed_own, away))
        here = feed_forward(normed_own, routing_own, weights, *shared)
        downward_token_rows, rank_rows = [
            one.astype(jnp.float32) + two.astype(jnp.float32) for one, two in zip(here, come)
        ]
    else:
        normed = lax.all_gather(normed_own, "tp", axis=0, tiled=True)
        downward_token_rows, rank_rows = [
            lax.psum_scatter(part_sum, "tp", scatter_dimension=0, tiled=True).astype(jnp.float32)
            for part_sum in feed_forward(normed, routing, weights, *shared)
        ]
    low_rank_product = jnp.dot(
        rank_rows.astype(jnp.bfloat16), down_expand, preferred_element_type=jnp.float32
    )
    return (
        after_attention_state + downward_token_rows + adapter_scale_factor * low_rank_product
    ).astype(jnp.bfloat16)


def solution(mesh):
    placed = (
        P("seq", "tp"),
        P("seq", "tp"),
        P("seq", "tp"),
        P(("seq", "tp"), None),
        P("tp", None),
        P(),
        P(),
        P("seq", "tp"),
        P("seq", "tp"),
        P("tp", "seq"),
        P(),
        P(),
        P(None, "tp"),
        P(None, "tp"),
        P("tp", None),
        P(),
        P("seq", None),
        P(),
    )
    return jax.shard_map(
        on_device, mesh=mesh, in_specs=placed, out_specs=P(("seq", "tp"), None), check_vma=False
    )
```

```python
import functools
import math

import jax
import jax.numpy as jnp
from jax import lax
from jax.experimental import pallas as pl
from jax.experimental.pallas import tpu as pltpu
from jax.sharding import PartitionSpec as P

HEAD = 128
EXPERTS = 8
RANK = 16
WINDOW = 4096


adapter_scale_factor = 2.0
epsilon = 1e-05
masked_score = -1e30


MESH = pl.DeviceIdType.MESH
KEY_TILE = 512
HIDDEN_TILE = 700


def greet_all(n, me):
    barrier = pltpu.get_barrier_semaphore()

    def greet(i, carry):
        pl.semaphore_signal(
            barrier, inc=1, device_id={"seq": lax.rem(me + i, n)}, device_id_type=MESH
        )
        return carry

    lax.fori_loop(1, n, greet, 0)
    pl.semaphore_wait(barrier, n - 1)


def spread_kernel(n, group, q_ref, kv_ref, q_out, kv_out, kv_s, kv_r, q_s, q_r, f_s, f_r, own_s, own_r, loc):
    me = lax.axis_index("seq")
    chips = n // 2
    chip, core = me // 2, lax.rem(me, 2)
    sib = chip * 2 + (1 - core)
    tokens = q_ref.shape[0]
    part = tokens // group
    greet_all(n, me)

    def rows(j):
        return pl.ds(pl.multiple_of(j * tokens, tokens), tokens)

    def q_rows(j):
        return pl.ds(pl.multiple_of(j * part, part), part)

    def cols(d):
        return pl.ds(pl.multiple_of((d // group) * HEAD, HEAD), HEAD)

    def kv_copy(kind, source, d, send, recv):
        return pltpu.make_async_remote_copy(
            src_ref=kv_ref.at[kind, :, cols(d)],
            dst_ref=kv_out.at[kind, rows(source), :],
            send_sem=send,
            recv_sem=recv,
            device_id={"seq": d},
            device_id_type=MESH,
        )

    def q_copy(source, d, send, recv):
        return pltpu.make_async_remote_copy(
            src_ref=q_ref.at[q_rows(lax.rem(d, group)), cols(d)],
            dst_ref=q_out.at[q_rows(source), :],
            send_sem=send,
            recv_sem=recv,
            device_id={"seq": d},
            device_id_type=MESH,
        )

    def forward(kind, source, send, recv):
        return pltpu.make_async_remote_copy(
            src_ref=kv_out.at[kind, rows(source), :],
            dst_ref=kv_out.at[kind, rows(source), :],
            send_sem=send,
            recv_sem=recv,
            device_id={"seq": sib},
            device_id_type=MESH,
        )

    def send(c, carry):
        for b in range(2):
            d = lax.rem(chip + c, chips) * 2 + b
            kv_copy(b, me, d, kv_s.at[c, b], kv_r.at[c, core]).start()
            q_copy(me, d, q_s.at[c, b], q_r.at[c, core]).start()
        return carry

    lax.fori_loop(1, chips, send, 0)
    for kind in range(2):
        kv_copy(kind, me, sib, own_s.at[kind], own_r.at[kind]).start()
    q_copy(me, sib, own_s.at[2], own_r.at[2]).start()
    local = [
        pltpu.make_async_copy(kv_ref.at[kind, :, cols(me)], kv_out.at[kind, rows(me), :], loc.at[kind])
        for kind in range(2)
    ]
    local.append(
        pltpu.make_async_copy(
            q_ref.at[q_rows(lax.rem(me, group)), cols(me)], q_out.at[q_rows(me), :], loc.at[2]
        )
    )
    for copy in local:
        copy.start()

    def pass_on(c, carry):
        for b in range(2):
            source = lax.rem(chip - c + chips, chips) * 2 + b
            kv_copy(core, source, sib, kv_s.at[c, b], kv_r.at[c, b]).wait_recv()
            forward(core, source, f_s.at[c, b], f_r.at[c, b]).start()
        return carry

    lax.fori_loop(1, chips, pass_on, 0)

    def finish(c, carry):
        for b in range(2):
            d = lax.rem(chip + c, chips) * 2 + b
            source = lax.rem(chip - c + chips, chips) * 2 + b
            kv_copy(b, me, d, kv_s.at[c, b], kv_r.at[c, core]).wait_send()
            q_copy(me, d, q_s.at[c, b], q_r.at[c, core]).wait_send()
            q_copy(source, sib, q_s.at[c, b], q_r.at[c, b]).wait_recv()
            forward(core, source, f_s.at[c, b], f_r.at[c, b]).wait_send()
            forward(1 - core, source, f_s.at[c, b], f_r.at[c, b]).wait_recv()
        return carry

    lax.fori_loop(1, chips, finish, 0)
    for kind in range(2):
        kv_copy(kind, me, sib, own_s.at[kind], own_r.at[kind]).wait_send()
        kv_copy(kind, sib, sib, own_s.at[kind], own_r.at[kind]).wait_recv()
    q_copy(me, sib, own_s.at[2], own_r.at[2]).wait_send()
    q_copy(sib, sib, own_s.at[2], own_r.at[2]).wait_recv()
    for copy in local:
        copy.wait()


def spread(n, group, queries, stacked):
    tokens = queries.shape[0]
    chips = n // 2
    dma = pltpu.SemaphoreType.DMA
    return pl.pallas_call(
        functools.partial(spread_kernel, n, group),
        out_shape=(
            jax.ShapeDtypeStruct((n * tokens // group, HEAD), queries.dtype),
            jax.ShapeDtypeStruct((2, n * tokens, HEAD), queries.dtype),
        ),
        in_specs=[pl.BlockSpec(memory_space=pl.ANY)] * 2,
        out_specs=(pl.BlockSpec(memory_space=pl.ANY),) * 2,
        scratch_shapes=[dma((chips, 2))] * 6 + [dma((3,))] * 3,
        compiler_params=pltpu.CompilerParams(collective_id=0, has_side_effects=True),
        cost_estimate=pl.CostEstimate(flops=0, bytes_accessed=200_000_000, transcendentals=0),
        name="spread_heads",
    )(queries, stacked)


def gather_kernel(n, tn, group, heads, rotate, x_ref, out_ref, s_sem, r_sem, loc):
    me, mt = lax.axis_index("seq"), lax.axis_index("tp")
    kept = out_ref.shape[0]
    part = kept * tn // group
    per = kept // part
    head, sub = me // group, lax.rem(me, group)
    owner = sub // per
    mine = owner == mt
    sources = tn * heads * per

    def source_of(i):
        t, h, q = i // (heads * per), lax.rem(i // per, heads), lax.rem(i, per)
        return h * group + mt * per + q, t

    def place(h, q, t, u):
        slot = lax.rem(t - u + tn, tn) if rotate else t
        return out_ref.at[
            pl.ds(pl.multiple_of(q * part, part), part),
            pl.ds(pl.multiple_of((slot * heads + h) * HEAD, HEAD), HEAD),
        ]

    def piece(d):
        return x_ref.at[pl.ds(pl.multiple_of(d * part, part), part), :]

    barrier = pltpu.get_barrier_semaphore()

    def greet(i, carry):
        s, t = source_of(i)

        @pl.when((s != me) | (t != mt))
        def _():
            pl.semaphore_signal(barrier, inc=1, device_id={"seq": s, "tp": t}, device_id_type=MESH)

        return carry

    lax.fori_loop(0, sources, greet, 0)
    pl.semaphore_wait(barrier, n - jnp.where(mine, 1, 0))
    own_id = (mt * heads + head) * per + lax.rem(sub, per)

    def send_copy(d):
        return pltpu.make_async_remote_copy(
            src_ref=piece(d),
            dst_ref=place(head, lax.rem(sub, per), mt, owner),
            send_sem=s_sem.at[d],
            recv_sem=r_sem.at[own_id],
            device_id={"seq": d, "tp": owner},
            device_id_type=MESH,
        )

    def receive(i):
        t, h, q = i // (heads * per), lax.rem(i // per, heads), lax.rem(i, per)
        return pltpu.make_async_remote_copy(
            src_ref=piece(me),
            dst_ref=place(h, q, t, mt),
            send_sem=s_sem.at[me],
            recv_sem=r_sem.at[i],
            device_id={"seq": lax.rem(me + 1, n), "tp": owner},
            device_id_type=MESH,
        )

    own = pltpu.make_async_copy(piece(me), place(head, lax.rem(sub, per), mt, mt), loc)

    def send(i, carry):
        send_copy(lax.rem(me + i, n)).start()
        return carry

    lax.fori_loop(1, n, send, 0)

    @pl.when(mine)
    def _():
        own.start()

    @pl.when(jnp.logical_not(mine))
    def _():
        send_copy(me).start()

    def sent(i, carry):
        send_copy(lax.rem(me + i, n)).wait_send()
        return carry

    lax.fori_loop(1, n, sent, 0)

    def arrive(i, carry):
        s, t = source_of(i)

        @pl.when((s != me) | (t != mt))
        def _():
            receive(i).wait_recv()

        return carry

    lax.fori_loop(0, sources, arrive, 0)

    @pl.when(mine)
    def _():
        own.wait()

    @pl.when(jnp.logical_not(mine))
    def _():
        send_copy(me).wait_send()


def regather(n, tn, group, heads, tokens, attended):
    dma = pltpu.SemaphoreType.DMA
    kept = tokens // tn
    part = tokens // group
    assert kept % part == 0
    return pl.pallas_call(
        functools.partial(gather_kernel, n, tn, group, heads, tn == 2),
        out_shape=jax.ShapeDtypeStruct((kept, tn * heads * HEAD), attended.dtype),
        in_specs=[pl.BlockSpec(memory_space=pl.ANY)],
        out_specs=pl.BlockSpec(memory_space=pl.ANY),
        scratch_shapes=[dma((n,)), dma((tn * heads * (kept // part),)), dma],
        compiler_params=pltpu.CompilerParams(collective_id=1, has_side_effects=True),
        cost_estimate=pl.CostEstimate(flops=0, bytes_accessed=60_000_000, transcendentals=0),
        name="regather_heads",
    )(attended)


def attend_kernel(tokens, part, docs, scalars, q_ref, k_ref, v_ref, o_ref):
    block = pl.program_id(0)
    first = block * tokens + scalars[docs] * part
    last = first + part - 1
    start = jnp.int32(0)
    q_pos = first + lax.broadcasted_iota(jnp.int32, (part, 1), 0)
    low = jnp.maximum(q_pos - (WINDOW - 1), 0)
    for j in range(docs):
        end = scalars[j]
        start = jnp.where(first >= end, end, start)
        low = jnp.maximum(low, jnp.where(q_pos >= end, end, 0))
    start = jnp.maximum(start, jnp.maximum(first - (WINDOW - 1), 0))
    q = q_ref[...]
    scale = 1.0 / math.sqrt(HEAD)

    def step(tile, carry):
        m, total, acc = carry
        base = pl.multiple_of(tile * KEY_TILE, KEY_TILE)
        k = k_ref[pl.ds(base, KEY_TILE), :]
        v = v_ref[pl.ds(base, KEY_TILE), :]
        scores = lax.dot_general(
            q, k, (((1,), (1,)), ((), ())), preferred_element_type=jnp.float32
        ) * scale
        k_pos = base + lax.broadcasted_iota(jnp.int32, (part, KEY_TILE), 1)
        scores = jnp.where((k_pos >= low) & (k_pos <= q_pos), scores, masked_score)
        new_m = jnp.maximum(m, jnp.max(scores, axis=1, keepdims=True))
        weights = jnp.exp(scores - new_m)
        shrink = jnp.exp(m - new_m)
        total = total * shrink + jnp.sum(weights, axis=1, keepdims=True)
        acc = acc * shrink + jnp.dot(
            weights.astype(jnp.bfloat16), v, preferred_element_type=jnp.float32
        )
        return new_m, total, acc

    _, total, acc = lax.fori_loop(
        start // KEY_TILE,
        last // KEY_TILE + 1,
        step,
        (
            jnp.full((part, 1), masked_score, jnp.float32),
            jnp.zeros((part, 1), jnp.float32),
            jnp.zeros((part, HEAD), jnp.float32),
        ),
    )
    o_ref[...] = (acc / total).astype(o_ref.dtype)


def attend(n, tokens, part, docs, scalars, q, kv):
    return pl.pallas_call(
        functools.partial(attend_kernel, tokens, part, docs),
        out_shape=jax.ShapeDtypeStruct(q.shape, q.dtype),
        grid_spec=pltpu.PrefetchScalarGridSpec(
            num_scalar_prefetch=1,
            grid=(n,),
            in_specs=[
                pl.BlockSpec((part, HEAD), lambda i, s: (i, 0)),
                pl.BlockSpec((None, n * tokens, HEAD), lambda i, s: (0, 0, 0)),
                pl.BlockSpec((None, n * tokens, HEAD), lambda i, s: (1, 0, 0)),
            ],
            out_specs=pl.BlockSpec((part, HEAD), lambda i, s: (i, 0)),
        ),
        compiler_params=pltpu.CompilerParams(vmem_limit_bytes=40 * 1024 * 1024),
        cost_estimate=pl.CostEstimate(
            flops=20_000_000_000, bytes_accessed=8_000_000, transcendentals=20_000_000
        ),
        name="attend_docs",
    )(scalars, q, kv, kv)


def dot_t(rows, other):
    return lax.dot_general(
        rows, other, (((1,), (1,)), ((), ())), preferred_element_type=jnp.float32
    )


def expert_kernel(tiles, x_ref, picked_ref, mix_ref, w_ref, gw_ref, uw_ref, ds_ref, out_ref, rank_ref, acc):
    tile = pl.program_id(0)
    x = x_ref[...]
    gate = dot_t(w_ref[0], x)
    up = dot_t(w_ref[1], x)
    mixed = 0.0
    ranks = []
    for slot in range(2):
        gate_one = gate + dot_t(gw_ref[...], picked_ref[slot])
        up_one = up + dot_t(uw_ref[...], picked_ref[2 + slot])
        hidden = jax.nn.silu(gate_one) * up_one
        mixed = mixed + mix_ref[slot : slot + 1, :] * hidden
        ranks.append(over_rows(hidden.astype(jnp.bfloat16), ds_ref[...]))
    down = over_rows(mixed.astype(jnp.bfloat16), w_ref[2])

    @pl.when(tile == 0)
    def _():
        acc[...] = down
        for slot in range(2):
            rank_ref[slot] = ranks[slot]

    @pl.when(tile > 0)
    def _():
        acc[...] += down
        for slot in range(2):
            rank_ref[slot] += ranks[slot]

    @pl.when(tile == tiles - 1)
    def _():
        out_ref[...] = acc[...].astype(out_ref.dtype)


def over_rows(one, other):
    return lax.dot_general(
        one, other, (((0,), (0,)), ((), ())), preferred_element_type=jnp.float32
    )


def expert_layers(x, picked, mix, weights, gate_widen, up_widen, down_shrink):
    rows, width = x.shape
    units, columns = down_shrink.shape
    size = max(
        [t for t in range(16, min(units, HIDDEN_TILE) + 1, 16) if units % t == 0], default=units
    )
    return pl.pallas_call(
        functools.partial(expert_kernel, units // size),
        out_shape=(
            jax.ShapeDtypeStruct((rows, width), jnp.bfloat16),
            jax.ShapeDtypeStruct((2, rows, columns), jnp.float32),
        ),
        grid=(units // size,),
        in_specs=[
            pl.BlockSpec((rows, width), lambda i: (0, 0)),
            pl.BlockSpec((4, rows, columns), lambda i: (0, 0, 0)),
            pl.BlockSpec((2, rows), lambda i: (0, 0)),
            pl.BlockSpec((3, size, width), lambda i: (0, i, 0)),
            pl.BlockSpec((size, columns), lambda i: (i, 0)),
            pl.BlockSpec((size, columns), lambda i: (i, 0)),
            pl.BlockSpec((size, columns), lambda i: (i, 0)),
        ],
        out_specs=(
            pl.BlockSpec((rows, width), lambda i: (0, 0)),
            pl.BlockSpec((2, rows, columns), lambda i: (0, 0, 0)),
        ),
        scratch_shapes=[pltpu.VMEM((rows, width), jnp.float32)],
        compiler_params=pltpu.CompilerParams(vmem_limit_bytes=48 * 1024 * 1024),
        cost_estimate=pl.CostEstimate(
            flops=6 * rows * width * units,
            bytes_accessed=6 * units * width,
            transcendentals=4 * rows * units,
        ),
        name="expert_layers",
    )(x, picked, mix, weights, gate_widen.T, up_widen.T, down_shrink)


def feed_forward(normed, routing, weights, router, gate_shrink, up_shrink, gate_widen_maps, upward_widen_maps, down_shrink):
    rank_gate = jnp.dot(normed, gate_shrink, preferred_element_type=jnp.float32).astype(
        jnp.bfloat16
    )
    rank_up = jnp.dot(normed, up_shrink, preferred_element_type=jnp.float32).astype(jnp.bfloat16)
    logits = jnp.dot(normed, router, preferred_element_type=jnp.float32)
    expert_ids = jnp.arange(EXPERTS, dtype=jnp.int32)
    first_logit = jnp.sum(jnp.where(routing[:, 0:1] == expert_ids[None, :], logits, 0.0), axis=1)
    second_logit = jnp.sum(jnp.where(routing[:, 1:2] == expert_ids[None, :], logits, 0.0), axis=1)
    weight_first = jax.nn.sigmoid(first_logit - second_logit)[:, None]
    weight_second = jax.nn.sigmoid(second_logit - first_logit)[:, None]
    column_expert = jnp.arange(EXPERTS * RANK, dtype=jnp.int32) // RANK
    pickers = [column_expert[None, :] == routing[:, slot : slot + 1] for slot in range(2)]
    picked = [
        jnp.where(picker, adapter_scale_factor * ranks, jnp.zeros_like(ranks))
        for ranks in (rank_gate, rank_up)
        for picker in pickers
    ]
    mix_weights = jnp.stack((weight_first[:, 0], weight_second[:, 0]))
    down_sum, shrunk = expert_layers(
        normed, jnp.stack(picked), mix_weights, weights, gate_widen_maps, upward_widen_maps, down_shrink
    )
    rank_down = weight_first * jnp.where(pickers[0], shrunk[0], 0.0) + weight_second * jnp.where(
        pickers[1], shrunk[1], 0.0
    )
    return down_sum, rank_down.astype(jnp.bfloat16)


def on_device(
    queries,
    keys,
    values,
    residual,
    out_weight,
    norm_gain,
    router,
    gate_weight,
    up_weight,
    down_weight,
    gate_shrink,
    up_shrink,
    gate_widen_maps,
    upward_widen_maps,
    down_shrink,
    down_expand,
    routing,
    doc_lengths,
):
    tokens_here = queries.shape[0]
    total_width = queries.shape[1]
    heads_here = total_width // HEAD
    seq_count = lax.axis_size("seq")
    group = seq_count // heads_here
    part = tokens_here // group
    seq_index = lax.axis_index("seq")
    tp_count = lax.axis_size("tp")
    weights = lax.all_gather(
        jnp.stack((gate_weight.T, up_weight.T, down_weight)), "seq", axis=2, tiled=True
    )
    stacked = jnp.stack((keys, values))
    head_queries, head_kv = spread(seq_count, group, queries, stacked)
    doc_ends = jnp.cumsum(doc_lengths)
    scalars = jnp.concatenate((doc_ends, lax.rem(seq_index, group)[None])).astype(jnp.int32)
    attended = attend(
        seq_count, tokens_here, part, doc_lengths.shape[0], scalars, head_queries, head_kv
    )
    attended = regather(seq_count, tp_count, group, heads_here, tokens_here, attended)
    if tp_count == 2:
        out_other = lax.ppermute(out_weight, "tp", [(0, 1), (1, 0)])
        projected = jnp.dot(
            attended[:, :total_width], out_weight, preferred_element_type=jnp.float32
        ) + jnp.dot(attended[:, total_width:], out_other, preferred_element_type=jnp.float32)
    else:
        projected = jnp.dot(
            attended,
            lax.all_gather(out_weight, "tp", axis=0, tiled=True),
            preferred_element_type=jnp.float32,
        )
    after_attention_state = residual.astype(jnp.float32) + projected
    mean_square = jnp.mean(after_attention_state * after_attention_state, axis=1, keepdims=True)
    normed_own = (after_attention_state * lax.rsqrt(mean_square + epsilon) * norm_gain).astype(
        jnp.bfloat16
    )
    shared = (router, gate_shrink, up_shrink, gate_widen_maps, upward_widen_maps, down_shrink)
    if tp_count == 2:
        swap = [(0, 1), (1, 0)]
        half = tokens_here // 2
        me = lax.axis_index("tp")
        normed_away = lax.ppermute(normed_own, "tp", swap)
        routing_own = lax.dynamic_slice_in_dim(routing, me * half, half, 0)
        routing_away = lax.dynamic_slice_in_dim(routing, (1 - me) * half, half, 0)
        away = feed_forward(normed_away, routing_away, weights, *shared)
        come = [lax.ppermute(part_sum, "tp", swap) for part_sum in away]
        normed_own, _ = lax.optimization_barrier((normed_own, away))
        here = feed_forward(normed_own, routing_own, weights, *shared)
        downward_token_rows, rank_rows = [
            one.astype(jnp.float32) + two.astype(jnp.float32) for one, two in zip(here, come)
        ]
    else:
        normed = lax.all_gather(normed_own, "tp", axis=0, tiled=True)
        downward_token_rows, rank_rows = [
            lax.psum_scatter(part_sum, "tp", scatter_dimension=0, tiled=True).astype(jnp.float32)
            for part_sum in feed_forward(normed, routing, weights, *shared)
        ]
    low_rank_product = jnp.dot(
        rank_rows.astype(jnp.bfloat16), down_expand, preferred_element_type=jnp.float32
    )
    return (
        after_attention_state + downward_token_rows + adapter_scale_factor * low_rank_product
    ).astype(jnp.bfloat16)


def solution(mesh):
    placed = (
        P("seq", "tp"),
        P("seq", "tp"),
        P("seq", "tp"),
        P(("seq", "tp"), None),
        P("tp", None),
        P(),
        P(),
        P("seq", "tp"),
        P("seq", "tp"),
        P("tp", "seq"),
        P(),
        P(),
        P(None, "tp"),
        P(None, "tp"),
        P("tp", None),
        P(),
        P("seq", None),
        P(),
    )
    return jax.shard_map(
        on_device, mesh=mesh, in_specs=placed, out_specs=P(("seq", "tp"), None), check_vma=False
    )
```

```python
import functools
import math

import jax
import jax.numpy as jnp
from jax import lax
from jax.experimental import pallas as pl
from jax.experimental.pallas import tpu as pltpu
from jax.sharding import PartitionSpec as P

HEAD = 128
EXPERTS = 8
RANK = 16
WINDOW = 4096


adapter_scale_factor = 2.0
epsilon = 1e-05
masked_score = -1e30


MESH = pl.DeviceIdType.MESH
KEY_TILE = 512
HIDDEN_TILE = 700


def greet_all(n, me):
    barrier = pltpu.get_barrier_semaphore()

    def greet(i, carry):
        pl.semaphore_signal(
            barrier, inc=1, device_id={"seq": lax.rem(me + i, n)}, device_id_type=MESH
        )
        return carry

    lax.fori_loop(1, n, greet, 0)
    pl.semaphore_wait(barrier, n - 1)


def spread_kernel(n, group, q_ref, kv_ref, q_out, kv_out, kv_s, kv_r, q_s, q_r, f_s, f_r, own_s, own_r, loc):
    me = lax.axis_index("seq")
    chips = n // 2
    chip, core = me // 2, lax.rem(me, 2)
    sib = chip * 2 + (1 - core)
    tokens = q_ref.shape[0]
    part = tokens // group
    greet_all(n, me)

    def rows(j):
        return pl.ds(pl.multiple_of(j * tokens, tokens), tokens)

    def q_rows(j):
        return pl.ds(pl.multiple_of(j * part, part), part)

    def cols(d):
        return pl.ds(pl.multiple_of((d // group) * HEAD, HEAD), HEAD)

    def kv_copy(kind, source, d, send, recv):
        return pltpu.make_async_remote_copy(
            src_ref=kv_ref.at[kind, :, cols(d)],
            dst_ref=kv_out.at[kind, rows(source), :],
            send_sem=send,
            recv_sem=recv,
            device_id={"seq": d},
            device_id_type=MESH,
        )

    def q_copy(source, d, send, recv):
        return pltpu.make_async_remote_copy(
            src_ref=q_ref.at[q_rows(lax.rem(d, group)), cols(d)],
            dst_ref=q_out.at[q_rows(source), :],
            send_sem=send,
            recv_sem=recv,
            device_id={"seq": d},
            device_id_type=MESH,
        )

    def forward(kind, source, send, recv):
        return pltpu.make_async_remote_copy(
            src_ref=kv_out.at[kind, rows(source), :],
            dst_ref=kv_out.at[kind, rows(source), :],
            send_sem=send,
            recv_sem=recv,
            device_id={"seq": sib},
            device_id_type=MESH,
        )

    def send(c, carry):
        for b in range(2):
            d = lax.rem(chip + c, chips) * 2 + b
            kv_copy(b, me, d, kv_s.at[c, b], kv_r.at[c, core]).start()
            q_copy(me, d, q_s.at[c, b], q_r.at[c, core]).start()
        return carry

    lax.fori_loop(1, chips, send, 0)
    for kind in range(2):
        kv_copy(kind, me, sib, own_s.at[kind], own_r.at[kind]).start()
    q_copy(me, sib, own_s.at[2], own_r.at[2]).start()
    local = [
        pltpu.make_async_copy(kv_ref.at[kind, :, cols(me)], kv_out.at[kind, rows(me), :], loc.at[kind])
        for kind in range(2)
    ]
    local.append(
        pltpu.make_async_copy(
            q_ref.at[q_rows(lax.rem(me, group)), cols(me)], q_out.at[q_rows(me), :], loc.at[2]
        )
    )
    for copy in local:
        copy.start()

    def pass_on(c, carry):
        for b in range(2):
            source = lax.rem(chip - c + chips, chips) * 2 + b
            kv_copy(core, source, sib, kv_s.at[c, b], kv_r.at[c, b]).wait_recv()
            forward(core, source, f_s.at[c, b], f_r.at[c, b]).start()
        return carry

    lax.fori_loop(1, chips, pass_on, 0)

    def finish(c, carry):
        for b in range(2):
            d = lax.rem(chip + c, chips) * 2 + b
            source = lax.rem(chip - c + chips, chips) * 2 + b
            kv_copy(b, me, d, kv_s.at[c, b], kv_r.at[c, core]).wait_send()
            q_copy(me, d, q_s.at[c, b], q_r.at[c, core]).wait_send()
            q_copy(source, sib, q_s.at[c, b], q_r.at[c, b]).wait_recv()
            forward(core, source, f_s.at[c, b], f_r.at[c, b]).wait_send()
            forward(1 - core, source, f_s.at[c, b], f_r.at[c, b]).wait_recv()
        return carry

    lax.fori_loop(1, chips, finish, 0)
    for kind in range(2):
        kv_copy(kind, me, sib, own_s.at[kind], own_r.at[kind]).wait_send()
        kv_copy(kind, sib, sib, own_s.at[kind], own_r.at[kind]).wait_recv()
    q_copy(me, sib, own_s.at[2], own_r.at[2]).wait_send()
    q_copy(sib, sib, own_s.at[2], own_r.at[2]).wait_recv()
    for copy in local:
        copy.wait()


def spread(n, group, queries, stacked):
    tokens = queries.shape[0]
    chips = n // 2
    dma = pltpu.SemaphoreType.DMA
    return pl.pallas_call(
        functools.partial(spread_kernel, n, group),
        out_shape=(
            jax.ShapeDtypeStruct((n * tokens // group, HEAD), queries.dtype),
            jax.ShapeDtypeStruct((2, n * tokens, HEAD), queries.dtype),
        ),
        in_specs=[pl.BlockSpec(memory_space=pl.ANY)] * 2,
        out_specs=(pl.BlockSpec(memory_space=pl.ANY),) * 2,
        scratch_shapes=[dma((chips, 2))] * 6 + [dma((3,))] * 3,
        compiler_params=pltpu.CompilerParams(collective_id=0, has_side_effects=True),
        cost_estimate=pl.CostEstimate(flops=0, bytes_accessed=200_000_000, transcendentals=0),
        name="spread_heads",
    )(queries, stacked)


def gather_kernel(n, tn, group, heads, rotate, x_ref, out_ref, s_sem, r_sem, loc):
    me, mt = lax.axis_index("seq"), lax.axis_index("tp")
    kept = out_ref.shape[0]
    part = kept * tn // group
    per = kept // part
    head, sub = me // group, lax.rem(me, group)
    owner = sub // per
    mine = owner == mt
    sources = tn * heads * per

    def source_of(i):
        t, h, q = i // (heads * per), lax.rem(i // per, heads), lax.rem(i, per)
        return h * group + mt * per + q, t

    def place(h, q, t, u):
        slot = lax.rem(t - u + tn, tn) if rotate else t
        return out_ref.at[
            pl.ds(pl.multiple_of(q * part, part), part),
            pl.ds(pl.multiple_of((slot * heads + h) * HEAD, HEAD), HEAD),
        ]

    def piece(d):
        return x_ref.at[pl.ds(pl.multiple_of(d * part, part), part), :]

    barrier = pltpu.get_barrier_semaphore()

    def greet(i, carry):
        s, t = source_of(i)

        @pl.when((s != me) | (t != mt))
        def _():
            pl.semaphore_signal(barrier, inc=1, device_id={"seq": s, "tp": t}, device_id_type=MESH)

        return carry

    lax.fori_loop(0, sources, greet, 0)
    pl.semaphore_wait(barrier, n - jnp.where(mine, 1, 0))
    own_id = (mt * heads + head) * per + lax.rem(sub, per)

    def send_copy(d):
        return pltpu.make_async_remote_copy(
            src_ref=piece(d),
            dst_ref=place(head, lax.rem(sub, per), mt, owner),
            send_sem=s_sem.at[d],
            recv_sem=r_sem.at[own_id],
            device_id={"seq": d, "tp": owner},
            device_id_type=MESH,
        )

    def receive(i):
        t, h, q = i // (heads * per), lax.rem(i // per, heads), lax.rem(i, per)
        return pltpu.make_async_remote_copy(
            src_ref=piece(me),
            dst_ref=place(h, q, t, mt),
            send_sem=s_sem.at[me],
            recv_sem=r_sem.at[i],
            device_id={"seq": lax.rem(me + 1, n), "tp": owner},
            device_id_type=MESH,
        )

    own = pltpu.make_async_copy(piece(me), place(head, lax.rem(sub, per), mt, mt), loc)

    def send(i, carry):
        send_copy(lax.rem(me + i, n)).start()
        return carry

    lax.fori_loop(1, n, send, 0)

    @pl.when(mine)
    def _():
        own.start()

    @pl.when(jnp.logical_not(mine))
    def _():
        send_copy(me).start()

    def sent(i, carry):
        send_copy(lax.rem(me + i, n)).wait_send()
        return carry

    lax.fori_loop(1, n, sent, 0)

    def arrive(i, carry):
        s, t = source_of(i)

        @pl.when((s != me) | (t != mt))
        def _():
            receive(i).wait_recv()

        return carry

    lax.fori_loop(0, sources, arrive, 0)

    @pl.when(mine)
    def _():
        own.wait()

    @pl.when(jnp.logical_not(mine))
    def _():
        send_copy(me).wait_send()


def regather(n, tn, group, heads, tokens, attended):
    dma = pltpu.SemaphoreType.DMA
    kept = tokens // tn
    part = tokens // group
    assert kept % part == 0
    return pl.pallas_call(
        functools.partial(gather_kernel, n, tn, group, heads, tn == 2),
        out_shape=jax.ShapeDtypeStruct((kept, tn * heads * HEAD), attended.dtype),
        in_specs=[pl.BlockSpec(memory_space=pl.ANY)],
        out_specs=pl.BlockSpec(memory_space=pl.ANY),
        scratch_shapes=[dma((n,)), dma((tn * heads * (kept // part),)), dma],
        compiler_params=pltpu.CompilerParams(collective_id=1, has_side_effects=True),
        cost_estimate=pl.CostEstimate(flops=0, bytes_accessed=60_000_000, transcendentals=0),
        name="regather_heads",
    )(attended)


def attend_kernel(tokens, part, docs, scalars, q_ref, k_ref, v_ref, o_ref):
    block = pl.program_id(0)
    first = block * tokens + scalars[docs] * part
    last = first + part - 1
    start = jnp.int32(0)
    q_pos = first + lax.broadcasted_iota(jnp.int32, (part, 1), 0)
    low = jnp.maximum(q_pos - (WINDOW - 1), 0)
    for j in range(docs):
        end = scalars[j]
        start = jnp.where(first >= end, end, start)
        low = jnp.maximum(low, jnp.where(q_pos >= end, end, 0))
    start = jnp.maximum(start, jnp.maximum(first - (WINDOW - 1), 0))
    q = q_ref[...]
    scale = 1.0 / math.sqrt(HEAD)

    def step(tile, carry):
        m, total, acc = carry
        base = pl.multiple_of(tile * KEY_TILE, KEY_TILE)
        k = k_ref[pl.ds(base, KEY_TILE), :]
        v = v_ref[pl.ds(base, KEY_TILE), :]
        scores = lax.dot_general(
            q, k, (((1,), (1,)), ((), ())), preferred_element_type=jnp.float32
        ) * scale
        k_pos = base + lax.broadcasted_iota(jnp.int32, (part, KEY_TILE), 1)
        scores = jnp.where((k_pos >= low) & (k_pos <= q_pos), scores, masked_score)
        new_m = jnp.maximum(m, jnp.max(scores, axis=1, keepdims=True))
        weights = jnp.exp(scores - new_m)
        shrink = jnp.exp(m - new_m)
        total = total * shrink + jnp.sum(weights, axis=1, keepdims=True)
        acc = acc * shrink + jnp.dot(
            weights.astype(jnp.bfloat16), v, preferred_element_type=jnp.float32
        )
        return new_m, total, acc

    _, total, acc = lax.fori_loop(
        start // KEY_TILE,
        last // KEY_TILE + 1,
        step,
        (
            jnp.full((part, 1), masked_score, jnp.float32),
            jnp.zeros((part, 1), jnp.float32),
            jnp.zeros((part, HEAD), jnp.float32),
        ),
    )
    o_ref[...] = (acc / total).astype(o_ref.dtype)


def attend(n, tokens, part, docs, scalars, q, kv):
    return pl.pallas_call(
        functools.partial(attend_kernel, tokens, part, docs),
        out_shape=jax.ShapeDtypeStruct(q.shape, q.dtype),
        grid_spec=pltpu.PrefetchScalarGridSpec(
            num_scalar_prefetch=1,
            grid=(n,),
            in_specs=[
                pl.BlockSpec((part, HEAD), lambda i, s: (i, 0)),
                pl.BlockSpec((None, n * tokens, HEAD), lambda i, s: (0, 0, 0)),
                pl.BlockSpec((None, n * tokens, HEAD), lambda i, s: (1, 0, 0)),
            ],
            out_specs=pl.BlockSpec((part, HEAD), lambda i, s: (i, 0)),
        ),
        compiler_params=pltpu.CompilerParams(vmem_limit_bytes=40 * 1024 * 1024),
        cost_estimate=pl.CostEstimate(
            flops=20_000_000_000, bytes_accessed=8_000_000, transcendentals=20_000_000
        ),
        name="attend_docs",
    )(scalars, q, kv, kv)


def dot_t(rows, other):
    return lax.dot_general(
        rows, other, (((1,), (1,)), ((), ())), preferred_element_type=jnp.float32
    )


def expert_kernel(tiles, x_ref, picked_ref, mix_ref, w_ref, gw_ref, uw_ref, ds_ref, out_ref, rank_ref, acc):
    tile = pl.program_id(0)
    x = x_ref[...]
    gate = dot_t(w_ref[0], x)
    up = dot_t(w_ref[1], x)
    mixed = 0.0
    ranks = []
    for slot in range(2):
        gate_one = gate + dot_t(gw_ref[...], picked_ref[slot])
        up_one = up + dot_t(uw_ref[...], picked_ref[2 + slot])
        hidden = jax.nn.silu(gate_one) * up_one
        mixed = mixed + mix_ref[slot : slot + 1, :] * hidden
        ranks.append(over_rows(hidden.astype(jnp.bfloat16), ds_ref[...]))
    down = over_rows(mixed.astype(jnp.bfloat16), w_ref[2])

    @pl.when(tile == 0)
    def _():
        acc[...] = down
        for slot in range(2):
            rank_ref[slot] = ranks[slot]

    @pl.when(tile > 0)
    def _():
        acc[...] += down
        for slot in range(2):
            rank_ref[slot] += ranks[slot]

    @pl.when(tile == tiles - 1)
    def _():
        out_ref[...] = acc[...].astype(out_ref.dtype)


def over_rows(one, other):
    return lax.dot_general(
        one, other, (((0,), (0,)), ((), ())), preferred_element_type=jnp.float32
    )


def expert_layers(x, picked, mix, weights, gate_widen, up_widen, down_shrink):
    rows, width = x.shape
    units, columns = down_shrink.shape
    size = max(
        [t for t in range(16, min(units, HIDDEN_TILE) + 1, 16) if units % t == 0], default=units
    )
    return pl.pallas_call(
        functools.partial(expert_kernel, units // size),
        out_shape=(
            jax.ShapeDtypeStruct((rows, width), jnp.bfloat16),
            jax.ShapeDtypeStruct((2, rows, columns), jnp.float32),
        ),
        grid=(units // size,),
        in_specs=[
            pl.BlockSpec((rows, width), lambda i: (0, 0)),
            pl.BlockSpec((4, rows, columns), lambda i: (0, 0, 0)),
            pl.BlockSpec((2, rows), lambda i: (0, 0)),
            pl.BlockSpec((3, size, width), lambda i: (0, i, 0)),
            pl.BlockSpec((size, columns), lambda i: (i, 0)),
            pl.BlockSpec((size, columns), lambda i: (i, 0)),
            pl.BlockSpec((size, columns), lambda i: (i, 0)),
        ],
        out_specs=(
            pl.BlockSpec((rows, width), lambda i: (0, 0)),
            pl.BlockSpec((2, rows, columns), lambda i: (0, 0, 0)),
        ),
        scratch_shapes=[pltpu.VMEM((rows, width), jnp.float32)],
        compiler_params=pltpu.CompilerParams(vmem_limit_bytes=63 * 1024 * 1024),
        cost_estimate=pl.CostEstimate(
            flops=6 * rows * width * units,
            bytes_accessed=6 * units * width,
            transcendentals=4 * rows * units,
        ),
        name="expert_layers",
    )(x, picked, mix, weights, gate_widen.T, up_widen.T, down_shrink)


def feed_forward(normed, routing, weights, router, gate_shrink, up_shrink, gate_widen_maps, upward_widen_maps, down_shrink, after=()):
    rank_gate = jnp.dot(normed, gate_shrink, preferred_element_type=jnp.float32).astype(
        jnp.bfloat16
    )
    rank_up = jnp.dot(normed, up_shrink, preferred_element_type=jnp.float32).astype(jnp.bfloat16)
    logits = jnp.dot(normed, router, preferred_element_type=jnp.float32)
    expert_ids = jnp.arange(EXPERTS, dtype=jnp.int32)
    first_logit = jnp.sum(jnp.where(routing[:, 0:1] == expert_ids[None, :], logits, 0.0), axis=1)
    second_logit = jnp.sum(jnp.where(routing[:, 1:2] == expert_ids[None, :], logits, 0.0), axis=1)
    weight_first = jax.nn.sigmoid(first_logit - second_logit)[:, None]
    weight_second = jax.nn.sigmoid(second_logit - first_logit)[:, None]
    column_expert = jnp.arange(EXPERTS * RANK, dtype=jnp.int32) // RANK
    pickers = [column_expert[None, :] == routing[:, slot : slot + 1] for slot in range(2)]
    picked = [
        jnp.where(picker, adapter_scale_factor * ranks, jnp.zeros_like(ranks))
        for ranks in (rank_gate, rank_up)
        for picker in pickers
    ]
    mix_weights = jnp.stack((weight_first[:, 0], weight_second[:, 0]))
    normed, _ = lax.optimization_barrier((normed, after))
    down_sum, shrunk = expert_layers(
        normed, jnp.stack(picked), mix_weights, weights, gate_widen_maps, upward_widen_maps, down_shrink
    )
    rank_down = weight_first * jnp.where(pickers[0], shrunk[0], 0.0) + weight_second * jnp.where(
        pickers[1], shrunk[1], 0.0
    )
    return down_sum, rank_down.astype(jnp.bfloat16)


def on_device(
    queries,
    keys,
    values,
    residual,
    out_weight,
    norm_gain,
    router,
    gate_weight,
    up_weight,
    down_weight,
    gate_shrink,
    up_shrink,
    gate_widen_maps,
    upward_widen_maps,
    down_shrink,
    down_expand,
    routing,
    doc_lengths,
):
    tokens_here = queries.shape[0]
    total_width = queries.shape[1]
    heads_here = total_width // HEAD
    seq_count = lax.axis_size("seq")
    group = seq_count // heads_here
    part = tokens_here // group
    seq_index = lax.axis_index("seq")
    tp_count = lax.axis_size("tp")
    weights = lax.all_gather(
        jnp.stack((gate_weight.T, up_weight.T, down_weight)), "seq", axis=2, tiled=True
    )
    stacked = jnp.stack((keys, values))
    head_queries, head_kv = spread(seq_count, group, queries, stacked)
    doc_ends = jnp.cumsum(doc_lengths)
    scalars = jnp.concatenate((doc_ends, lax.rem(seq_index, group)[None])).astype(jnp.int32)
    attended = attend(
        seq_count, tokens_here, part, doc_lengths.shape[0], scalars, head_queries, head_kv
    )
    attended = regather(seq_count, tp_count, group, heads_here, tokens_here, attended)
    if tp_count == 2:
        out_other = lax.ppermute(out_weight, "tp", [(0, 1), (1, 0)])
        projected = jnp.dot(
            attended[:, :total_width], out_weight, preferred_element_type=jnp.float32
        ) + jnp.dot(attended[:, total_width:], out_other, preferred_element_type=jnp.float32)
    else:
        projected = jnp.dot(
            attended,
            lax.all_gather(out_weight, "tp", axis=0, tiled=True),
            preferred_element_type=jnp.float32,
        )
    after_attention_state = residual.astype(jnp.float32) + projected
    mean_square = jnp.mean(after_attention_state * after_attention_state, axis=1, keepdims=True)
    normed_own = (after_attention_state * lax.rsqrt(mean_square + epsilon) * norm_gain).astype(
        jnp.bfloat16
    )
    shared = (router, gate_shrink, up_shrink, gate_widen_maps, upward_widen_maps, down_shrink)
    if tp_count == 2:
        swap = [(0, 1), (1, 0)]
        half = tokens_here // 2
        me = lax.axis_index("tp")
        normed_away = lax.ppermute(normed_own, "tp", swap)
        routing_own = lax.dynamic_slice_in_dim(routing, me * half, half, 0)
        routing_away = lax.dynamic_slice_in_dim(routing, (1 - me) * half, half, 0)
        away = feed_forward(normed_away, routing_away, weights, *shared)
        come = [lax.ppermute(part_sum, "tp", swap) for part_sum in away]
        here = feed_forward(normed_own, routing_own, weights, *shared, after=away)
        downward_token_rows, rank_rows = [
            one.astype(jnp.float32) + two.astype(jnp.float32) for one, two in zip(here, come)
        ]
    else:
        normed = lax.all_gather(normed_own, "tp", axis=0, tiled=True)
        downward_token_rows, rank_rows = [
            lax.psum_scatter(part_sum, "tp", scatter_dimension=0, tiled=True).astype(jnp.float32)
            for part_sum in feed_forward(normed, routing, weights, *shared)
        ]
    low_rank_product = jnp.dot(
        rank_rows.astype(jnp.bfloat16), down_expand, preferred_element_type=jnp.float32
    )
    return (
        after_attention_state + downward_token_rows + adapter_scale_factor * low_rank_product
    ).astype(jnp.bfloat16)


def solution(mesh):
    placed = (
        P("seq", "tp"),
        P("seq", "tp"),
        P("seq", "tp"),
        P(("seq", "tp"), None),
        P("tp", None),
        P(),
        P(),
        P("seq", "tp"),
        P("seq", "tp"),
        P("tp", "seq"),
        P(),
        P(),
        P(None, "tp"),
        P(None, "tp"),
        P("tp", None),
        P(),
        P("seq", None),
        P(),
    )
    return jax.shard_map(
        on_device, mesh=mesh, in_specs=placed, out_specs=P(("seq", "tp"), None), check_vma=False
    )
```
